128 devices in a mesh: box: 32 (over y, z, core), tx: 4 (over x).
Axes of the slice: x: 4, y: 4, z: 4, core: 2. Of those that a mesh axis runs over, the one named last changes fastest.
Arguments:
- bank: bfloat16 [512, 1024, 1024], P('box', 'tx'), may hold values from -6 to 6
- pick: int32 [64], replicated, may hold values from 0 to 1023, as said below
- slot_box: int32 [512], replicated, may hold values from 0 to 511, each once
- leaf_factor: bfloat16 [512, 512, 128], P('box'), may hold values from -0.1875 to 0.1875
- self_factor: bfloat16 [9, 512, 64, 128], P(None, 'box'), may hold values from -0.375 to 0.375
- cross_factor: bfloat16 [9, 512, 64, 128], P(None, 'box'), may hold values from -0.375 to 0.375
- target_factor: bfloat16 [512, 64, 4096], P('box'), may hold values from -0.5 to 0.5
Outputs:
- field: bfloat16 [512, 64, 4096], P('box', 'tx')
The draws below stay inside these ranges and needn't reach their ends.
Inputs may be any that keep to these rules, and one draw needn't show every extreme that they name: `pick`: distinct stored transmitters. `slot_box`: each box once.
All inputs are finite; a program needn't handle non-finite values.
Results may differ from the reference program's by a relative error of at most 0.023.
Values may be sent and summed in bfloat16 or wider, within the bound.
A program may use at most 128 MiB of HBM per device.

```python
import jax
import jax.numpy as jnp

NB = 512
LEVELS = 9
K = 64
UNK = 512
PTS = 2048
TXC = 64
BANK = 1024


def draw_pick(key, part):
    first_key = jax.random.fold_in(key, 11)
    second_key = jax.random.fold_in(key, 12)
    middle = jax.random.permutation(first_key, BANK - 2)[:TXC - 2] + 1
    joined = jnp.concatenate([jnp.array([0, BANK - 1], dtype=jnp.int32), middle.astype(jnp.int32)])
    order = jax.random.permutation(second_key, TXC)
    return joined[order].astype(jnp.int32)


def block_scale(key, dims, cuts, low, largest):
    level, own = 1.0, jax.random.fold_in(key, 6)
    for dim, blocks in cuts:
        heights = jnp.exp(jax.random.uniform(jax.random.fold_in(own, dim), (blocks,), jnp.float32, low / len(cuts), largest / len(cuts)))
        level = level * jnp.repeat(heights, dims[dim] // blocks).reshape([-1 if axis == dim else 1 for axis in range(len(dims))])
    return level


def bell_draw(stream_key, extent, width, reach, cuts=(), kind=jnp.bfloat16):
    loudness = block_scale(stream_key, extent, cuts, -0.22, 0.18) if cuts else 1.0
    result = jax.random.normal(stream_key, extent, jnp.float32) * width * loudness
    return jnp.minimum(jnp.maximum(result, -reach), reach).astype(kind)


def setup_inputs(seed: int = 0) -> dict:
    key_of = jax.random.split(jax.random.key(seed), 8)
    bank = bell_draw(key_of[0], (NB, BANK, 2 * UNK), 1.0, 6.0, ((0, 32), (1, 4)))
    pick = draw_pick(jax.random.fold_in(key_of[7], 71), 0)
    slot_box = jax.random.permutation(key_of[2], NB).astype(jnp.int32)
    leaf_factor = bell_draw(key_of[3], (NB, UNK, 2 * K), (2 * UNK) ** -0.5, 0.1875, ((0, 32),))
    self_factor = bell_draw(key_of[4], (LEVELS, NB, K, 2 * K), (4 * K) ** -0.5, 0.375, ((1, 32),))
    cross_factor = bell_draw(key_of[5], (LEVELS, NB, K, 2 * K), (4 * K) ** -0.5, 0.375, ((1, 32),))
    target_factor = bell_draw(key_of[6], (NB, K, 2 * PTS), (2 * K) ** -0.5, 0.5, ((0, 32),))
    return dict(bank=bank, pick=pick, slot_box=slot_box, leaf_factor=leaf_factor, self_factor=self_factor, cross_factor=cross_factor, target_factor=target_factor)


def complex_times(values, matrix):
    inner = matrix.shape[-2]
    half = matrix.shape[-1] // 2
    mat = matrix.astype(jnp.float32)
    first = jnp.einsum("brn,bnk->brk", values[..., :inner].astype(jnp.float32), mat)
    second = jnp.einsum("brn,bnk->brk", values[..., inner:].astype(jnp.float32), mat)
    return jnp.concatenate([first[..., :half] - second[..., half:], first[..., half:] + second[..., :half]], axis=-1)


def reference(bank, pick, slot_box, leaf_factor, self_factor, cross_factor, target_factor):
    selected = jnp.take(bank, pick, axis=1)
    coefs = complex_times(selected, leaf_factor).astype(jnp.bfloat16)
    current = jnp.take(coefs, slot_box, axis=0)
    slots = jnp.arange(NB, dtype=jnp.int32)
    for level in range(LEVELS):
        partner = jnp.take(current, jnp.bitwise_xor(slots, 1 << level), axis=0)
        mixed = complex_times(current, self_factor[level]) + complex_times(partner, cross_factor[level])
        current = mixed.astype(jnp.bfloat16)
    return complex_times(current, target_factor).astype(jnp.bfloat16)
```

```python
import functools

import jax
import jax.numpy as jnp
from jax import lax
from jax.experimental import pallas as pl
from jax.experimental.pallas import tpu as pltpu
from jax.sharding import PartitionSpec as P

MESH = pl.DeviceIdType.MESH
GROUPS = 4


def half_routes():
    routes = {}
    for half, (first, second) in enumerate((("z", "y"), ("y", "z"))):
        unit = {"y": (1, 0), "z": (0, 1)}
        e1, e2 = unit[first], unit[second]
        at = lambda i, j: (i * e1[0] + j * e2[0], i * e1[1] + j * e2[1])
        base = half * 8
        full, low, high = (base, 8), (base, 4), (base + 4, 4)
        routes[half, "T1L"] = (at(-1, 0), full, first, -1)
        routes[half, "T1R"] = (at(1, 0), full, first, 1)
        routes[half, "T2L"] = (at(2, 0), low, first, -1)
        routes[half, "T2R"] = (at(2, 0), high, first, 1)
        for i in (0, -1, 1, 2):
            routes[half, "U1L", i] = (at(i, -1), full, second, -1)
            routes[half, "U1R", i] = (at(i, 1), full, second, 1)
            routes[half, "U2L", i] = (at(i, 2), low, second, -1)
            routes[half, "U2R", i] = (at(i, 2), high, second, 1)
    return routes


ROUTES = half_routes()
ROUTE_ID = {name: i for i, name in enumerate(ROUTES)}


def gather_levels_kernel(
    pick_ref, slot_ref, bank_ref, leaf_ref, self_ref, cross_ref, out_ref,
    bank_buf, leaf_buf, weights, part_send, part_recv, pool, core_send, core_recv, state, partner,
    bank_sem, leaf_sem, weight_sem, part_ssem, part_rsem, pool_ssem, pool_rsem,
    core_ssem, core_rsem, level_ssem, level_rsem,
):
    boxes = bank_ref.shape[0]
    stored = bank_ref.shape[1]
    columns = pick_ref.shape[0]
    own_cols = columns // 4
    levels = self_ref.shape[0]
    me = lax.axis_index("box")
    tx = lax.axis_index("tx")
    y = me // 8
    z = (me // 2) % 4
    core = me % 2

    def box_at(yy, zz, cc):
        return yy * 8 + zz * 2 + cc

    def chip_at(dy, dz):
        return ((y + dy + 4) % 4) * 4 + (z + dz + 4) % 4

    def device_at(dy, dz):
        return box_at((y + dy + 4) % 4, (z + dz + 4) % 4, core), tx

    core_mate = (box_at(y, z, 1 - core), tx)
    mates = [
        core_mate,
        (box_at(y, z + 1 - 2 * (z % 2), core), tx),
        device_at(0, 2),
        (box_at(y + 1 - 2 * (y % 2), z, core), tx),
        device_at(2, 0),
    ]
    tx_mates = [(me, (tx + d) % 4) for d in (1, 2, 3)]

    bank_in = [pltpu.make_async_copy(bank_ref.at[b], bank_buf.at[b], bank_sem.at[b]) for b in range(boxes)]
    leaf_in = [
        pltpu.make_async_copy(leaf_ref.at[pl.ds(4 * g, 4)], leaf_buf.at[pl.ds(4 * g, 4)], leaf_sem.at[g])
        for g in range(boxes // 4)
    ]
    for g in range(boxes // 4):
        leaf_in[g].start()
        for b in range(4 * g, 4 * g + 4):
            bank_in[b].start()
    weights_in = []
    for l in range(levels):
        weights_in.append((
            pltpu.make_async_copy(self_ref.at[l], weights.at[l, :, pl.ds(0, 64), :], weight_sem.at[l, 0]),
            pltpu.make_async_copy(cross_ref.at[l], weights.at[l, :, pl.ds(64, 64), :], weight_sem.at[l, 1]),
        ))
        for copy in weights_in[-1]:
            copy.start()

    barrier = pltpu.get_barrier_semaphore()
    greeted = tx_mates + [device_at(0, 1), device_at(0, 3), device_at(1, 0), device_at(3, 0),
                          device_at(0, 2), device_at(2, 0), core_mate]
    for dev in greeted:
        pl.semaphore_signal(barrier, inc=1, device_id=dev, device_id_type=MESH)

    lane = lax.broadcasted_iota(jnp.int32, (8, stored), 1)
    row = lax.broadcasted_iota(jnp.int32, (8, stored), 0)
    tiles = []
    for g in range(columns // 8):
        want = jnp.full((8, stored), -1, jnp.int32)
        for i in range(8):
            want = jnp.where(row == i, pick_ref[8 * g + i] - tx * stored, want)
        tiles.append(jnp.where(want == lane, 1.0, 0.0).astype(jnp.float32))
    chooser = jnp.concatenate(tiles, axis=0).astype(jnp.bfloat16)

    def turned(r, rows):
        lanes = lax.broadcasted_iota(jnp.int32, (rows, 128), 1)
        second = pltpu.roll(r[rows:], 64, axis=1)
        return r[:rows] + jnp.where(lanes < 64, -second, second)

    def leaf_of(b):
        chosen = jnp.dot(chooser, bank_buf[b], preferred_element_type=jnp.float32).astype(jnp.bfloat16)
        half = chosen.shape[1] // 2
        both = jnp.concatenate([chosen[:, :half], chosen[:, half:]], axis=0)
        r = jnp.dot(both, leaf_buf[b], preferred_element_type=jnp.float32)
        coefs = turned(r, columns).astype(jnp.bfloat16)
        for t in range(4):
            part_send[t, b] = coefs[t * own_cols:(t + 1) * own_cols]

    def part_copy(h, d):
        to = (tx + d) % 4
        return pltpu.make_async_remote_copy(
            part_send.at[to, pl.ds(8 * h, 8)], part_recv.at[d - 1, pl.ds(8 * h, 8)],
            part_ssem.at[h, d - 1], part_rsem.at[h, d - 1],
            device_id=(me, to), device_id_type=MESH)

    for g in range(boxes // 4):
        leaf_in[g].wait()
        for b in range(4 * g, 4 * g + 4):
            bank_in[b].wait()
        for b in range(4 * g, 4 * g + 4):
            leaf_of(b)
        if g == 1:
            pl.semaphore_wait(barrier, len(greeted))
        if g % 2 == 1:
            for d in (1, 3, 2):
                part_copy(g // 2, d).start()

    def route_copy(name, sending):
        (dy, dz), (first, count), axis, side = ROUTES[name]
        step = (side, 0) if axis == "y" else (0, side)
        if sending:
            item = (dy - step[0], dz - step[1])
            dev = device_at(-step[0], -step[1])
        else:
            item = (dy, dz)
            dev = device_at(step[0], step[1])
        start = chip_at(item[0], item[1]) * boxes + first
        where = pool.at[pl.ds(start, count)]
        k = ROUTE_ID[name]
        return pltpu.make_async_remote_copy(
            where, where, pool_ssem.at[k], pool_rsem.at[k], device_id=dev, device_id_type=MESH)

    def send(*names):
        for name in names:
            route_copy(name, True).start()

    def arrived(name):
        route_copy(name, False).wait_recv()

    mine = chip_at(0, 0) * boxes
    for h in (0, 1):
        for d in (1, 3, 2):
            part_copy(h, d).wait_recv()
        total = part_send[tx, pl.ds(8 * h, 8)].astype(jnp.float32)
        for d in range(3):
            total = total + part_recv[d, pl.ds(8 * h, 8)].astype(jnp.float32)
        pool[pl.ds(mine + 8 * h, 8)] = total.astype(jnp.bfloat16)
        send((h, "T1L"), (h, "T1R"), (h, "U1L", 0), (h, "U1R", 0))
    for h in (0, 1):
        arrived((h, "T1L"))
        send((h, "T2L"), (h, "U1L", -1), (h, "U1R", -1))
        arrived((h, "T1R"))
        send((h, "T2R"), (h, "U1L", 1), (h, "U1R", 1))
    for h in (0, 1):
        arrived((h, "U1L", 0))
        send((h, "U2L", 0))
        arrived((h, "U1R", 0))
        send((h, "U2R", 0))
    for h in (0, 1):
        arrived((h, "T2L"))
        arrived((h, "T2R"))
        send((h, "U1L", 2), (h, "U1R", 2))
    for i in (-1, 1, 2):
        for h in (0, 1):
            arrived((h, "U1L", i))
            send((h, "U2L", i))
            arrived((h, "U1R", i))
            send((h, "U2R", i))
    for i in (0, -1, 1, 2):
        for h in (0, 1):
            arrived((h, "U2L", i))
            arrived((h, "U2R", i))

    def chosen_box(slot):
        box = slot_ref[slot]
        dev = lax.shift_right_logical(box, 4)
        at = lax.shift_right_logical(dev, 1) * boxes + jnp.bitwise_and(box, 15)
        here = jnp.where(jnp.bitwise_and(dev, 1) == core, 1.0, 0.0).astype(jnp.float32)
        return pool[at].astype(jnp.float32) * here

    for s in range(boxes):
        core_send[s] = chosen_box(core_mate[0] * boxes + s).astype(jnp.bfloat16)
    core_copy = pltpu.make_async_remote_copy(
        core_send, core_recv, core_ssem, core_rsem, device_id=core_mate, device_id_type=MESH)
    core_copy.start()
    own = [chosen_box(me * boxes + s) for s in range(boxes)]
    core_copy.wait_recv()
    for s in range(boxes):
        state[0, s] = (own[s] + core_recv[s].astype(jnp.float32)).astype(jnp.bfloat16)

    local = boxes.bit_length() - 1
    per = boxes // GROUPS

    def level_copy(l, g):
        k = (l - local) * GROUPS + g
        return pltpu.make_async_remote_copy(
            state.at[l, pl.ds(per * g, per)], partner.at[l - local, pl.ds(per * g, per)],
            level_ssem.at[k], level_rsem.at[k], device_id=mates[l - local], device_id_type=MESH)

    lanes = lax.broadcasted_iota(jnp.int32, (own_cols, 128), 1)
    for l in range(levels):
        for copy in weights_in[l]:
            copy.wait()
        for g in range(GROUPS):
            if l >= local:
                level_copy(l, g).wait_recv()
            for s in range(per * g, per * g + per):
                a = state[l, s].astype(jnp.float32)
                b = (state[l, s ^ (1 << l)] if l < local else partner[l - local, s]).astype(jnp.float32)
                real = jnp.where(lanes < 64, a, pltpu.roll(b, 64, axis=1))
                imag = jnp.where(lanes < 64, pltpu.roll(a, 64, axis=1), b)
                both = jnp.concatenate([real, imag], axis=0).astype(jnp.bfloat16)
                r = jnp.dot(both, weights[l, s], preferred_element_type=jnp.float32)
                new = turned(r, own_cols).astype(jnp.bfloat16)
                if l + 1 < levels:
                    state[l + 1, s] = new
                else:
                    out_ref[s] = new
            if local <= l + 1 < levels:
                level_copy(l + 1, g).start()

    for h in (0, 1):
        for d in (1, 2, 3):
            part_copy(h, d).wait_send()
    for name in ROUTES:
        route_copy(name, True).wait_send()
    core_copy.wait_send()
    for l in range(local, levels):
        for g in range(GROUPS):
            level_copy(l, g).wait_send()


def gather_levels(pick, slot_box, bank, leaf_factor, self_factor, cross_factor):
    boxes, stored, width = bank.shape
    levels = self_factor.shape[0]
    cols = pick.shape[0] // 4
    bf16 = jnp.bfloat16
    dma = pltpu.SemaphoreType.DMA
    anyspace = pl.BlockSpec(memory_space=pltpu.HBM)
    smem = pl.BlockSpec(memory_space=pltpu.SMEM)
    local = boxes.bit_length() - 1
    return pl.pallas_call(
        gather_levels_kernel,
        out_shape=jax.ShapeDtypeStruct((boxes, cols, 128), bf16),
        in_specs=[smem, smem, anyspace, anyspace, anyspace, anyspace],
        out_specs=pl.BlockSpec(memory_space=pltpu.VMEM),
        scratch_shapes=[
            pltpu.VMEM((boxes, stored, width), bf16),
            pltpu.VMEM(leaf_factor.shape, bf16),
            pltpu.VMEM((levels, boxes, 128, 128), bf16),
            pltpu.VMEM((4, boxes, cols, 128), bf16),
            pltpu.VMEM((3, boxes, cols, 128), bf16),
            pltpu.VMEM((16 * boxes, cols, 128), bf16),
            pltpu.VMEM((boxes, cols, 128), bf16),
            pltpu.VMEM((boxes, cols, 128), bf16),
            pltpu.VMEM((levels, boxes, cols, 128), bf16),
            pltpu.VMEM((levels - local, boxes, cols, 128), bf16),
            dma((boxes,)), dma((boxes // 4,)), dma((levels, 2)),
            dma((2, 3)), dma((2, 3)), dma((len(ROUTES),)), dma((len(ROUTES),)),
            dma, dma, dma(((levels - local) * GROUPS,)), dma(((levels - local) * GROUPS,)),
        ],
        compiler_params=pltpu.CompilerParams(
            collective_id=0, has_side_effects=True, vmem_limit_bytes=36 << 20),
        name="gather_levels",
    )(pick, slot_box, bank, leaf_factor, self_factor, cross_factor)


def target_kernel(x_ref, t_ref, o_ref):
    for s in range(x_ref.shape[0]):
        x = x_ref[s].astype(jnp.float32)
        both = jnp.concatenate([x, pltpu.roll(x, 64, axis=1)], axis=0)[:, :64].astype(jnp.bfloat16)
        rows = x.shape[0]
        half = t_ref.shape[2] // 2
        r = jnp.dot(both, t_ref[s], preferred_element_type=jnp.float32)
        o_ref[s, :, :half] = (r[:rows, :half] - r[rows:, half:]).astype(jnp.bfloat16)
        o_ref[s, :, half:] = (r[:rows, half:] + r[rows:, :half]).astype(jnp.bfloat16)


def target_map(x, target_factor):
    boxes, cols, _ = x.shape
    k, width = target_factor.shape[1:]
    step = 4
    return pl.pallas_call(
        target_kernel,
        out_shape=jax.ShapeDtypeStruct((boxes, cols, width), jnp.bfloat16),
        grid=(boxes // step,),
        in_specs=[
            pl.BlockSpec((step, cols, 128), lambda i: (i, 0, 0)),
            pl.BlockSpec((step, k, width), lambda i: (i, 0, 0)),
        ],
        out_specs=pl.BlockSpec((step, cols, width), lambda i: (i, 0, 0)),
        compiler_params=pltpu.CompilerParams(vmem_limit_bytes=16 << 20),
        name="target_map",
    )(x, target_factor)


def per_device(bank, pick, slot_box, leaf_factor, self_factor, cross_factor, target_factor):
    x = gather_levels(pick, slot_box, bank, leaf_factor, self_factor, cross_factor)
    return target_map(x, target_factor)


def solution(mesh):
    in_specs = (
        P("box", "tx", None),
        P(),
        P(),
        P("box", None, None),
        P(None, "box", None, None),
        P(None, "box", None, None),
        P("box", None, None),
    )
    out_specs = P("box", "tx", None)
    return jax.shard_map(
        per_device, mesh=mesh, in_specs=in_specs, out_specs=out_specs, check_vma=False
    )
```

```python
import functools

import jax
import jax.numpy as jnp
from jax import lax
from jax.experimental import pallas as pl
from jax.experimental.pallas import tpu as pltpu
from jax.sharding import PartitionSpec as P

MESH = pl.DeviceIdType.MESH
GROUPS = 4
CHUNKS = 4
VMEM_MIB = 54
SIDES = (2, 1, 3)


def coefs_kernel(
    pick_ref, slot_ref, bank_ref, leaf_ref, self_ref, cross_ref, out_ref,
    picks, slots, bank_buf, leaf_buf, weights, part_send, part_recv, pool, core_send, core_recv,
    state, partner,
    index_sem, bank_sem, leaf_sem, weight_sem, part_ssem, part_rsem, ring_ssem, ring_rsem, cross_ssem, cross_rsem,
    core_ssem, core_rsem, level_ssem, level_rsem,
):
    boxes, stored = bank_ref.shape[:2]
    columns = pick_ref.shape[0]
    own_cols = columns // 4
    levels = self_ref.shape[0]
    chunk = boxes // CHUNKS
    per = boxes // GROUPS
    local = boxes.bit_length() - 1
    me = lax.axis_index("box")
    tx = lax.axis_index("tx")
    y = me // 8
    z = (me // 2) % 4
    core = me % 2

    def chip_at(dy, dz):
        return ((y + dy) % 4) * 4 + (z + dz) % 4

    def device_at(dy, dz):
        return ((y + dy) % 4) * 8 + ((z + dz) % 4) * 2 + core, tx

    core_mate = (y * 8 + z * 2 + 1 - core, tx)
    mates = [
        core_mate,
        device_at(0, 1 + 2 * (z % 2)),
        device_at(0, 2),
        device_at(1 + 2 * (y % 2), 0),
        device_at(2, 0),
    ]

    barrier = pltpu.get_barrier_semaphore()
    greeted = ([(me, (tx + d) % 4) for d in SIDES] + [device_at(0, d) for d in SIDES]
               + [device_at(d, 0) for d in SIDES] + [core_mate])
    for dev in greeted:
        pl.semaphore_signal(barrier, inc=1, device_id=dev, device_id_type=MESH)

    index_in = [
        pltpu.make_async_copy(pick_ref, picks, index_sem.at[0]),
        pltpu.make_async_copy(slot_ref, slots, index_sem.at[1]),
    ]
    bank_in = [pltpu.make_async_copy(bank_ref.at[b], bank_buf.at[b], bank_sem.at[b]) for b in range(boxes)]
    leaf_in = [
        pltpu.make_async_copy(
            leaf_ref.at[pl.ds(chunk * g, chunk)], leaf_buf.at[pl.ds(chunk * g, chunk)], leaf_sem.at[g])
        for g in range(CHUNKS)
    ]
    weights_in = [
        (pltpu.make_async_copy(self_ref.at[l], weights.at[l, :, pl.ds(0, 64), :], weight_sem.at[l, 0]),
         pltpu.make_async_copy(cross_ref.at[l], weights.at[l, :, pl.ds(64, 64), :], weight_sem.at[l, 1]))
        for l in range(levels)
    ]
    for copy in index_in:
        copy.start()
    for g in range(CHUNKS):
        leaf_in[g].start()
        for b in range(chunk * g, chunk * g + chunk):
            bank_in[b].start()

    for copy in index_in:
        copy.wait()
    lane = lax.broadcasted_iota(jnp.int32, (8, stored), 1)
    row = lax.broadcasted_iota(jnp.int32, (8, stored), 0)
    tiles = []
    for g in range(columns // 8):
        want = jnp.full((8, stored), -1, jnp.int32)
        for i in range(8):
            want = jnp.where(row == i, picks[8 * g + i] - tx * stored, want)
        tiles.append(jnp.where(want == lane, 1.0, 0.0).astype(jnp.float32))
    chooser = jnp.concatenate(tiles, axis=0).astype(jnp.bfloat16)

    def turned(r, rows):
        lanes = lax.broadcasted_iota(jnp.int32, (rows, 128), 1)
        second = pltpu.roll(r[rows:], 64, axis=1)
        return r[:rows] + jnp.where(lanes < 64, -second, second)

    def leaf_of(b):
        chosen = jnp.dot(chooser, bank_buf[b], preferred_element_type=jnp.float32).astype(jnp.bfloat16)
        half = chosen.shape[1] // 2
        both = jnp.concatenate([chosen[:, :half], chosen[:, half:]], axis=0)
        r = jnp.dot(both, leaf_buf[b], preferred_element_type=jnp.float32)
        coefs = turned(r, columns).astype(jnp.bfloat16)
        for t in range(4):
            part_send[t, b] = coefs[t * own_cols:(t + 1) * own_cols]

    def part_copy(h, d):
        to = (tx + d) % 4
        return pltpu.make_async_remote_copy(
            part_send.at[to, pl.ds(chunk * h, chunk)], part_recv.at[d - 1, pl.ds(chunk * h, chunk)],
            part_ssem.at[h, d - 1], part_rsem.at[h, d - 1],
            device_id=(me, to), device_id_type=MESH)

    for h in range(CHUNKS):
        leaf_in[h].wait()
        for b in range(chunk * h, chunk * h + chunk):
            bank_in[b].wait()
        for b in range(chunk * h, chunk * h + chunk):
            leaf_of(b)
        if h == CHUNKS - 1:
            pl.semaphore_wait(barrier, len(greeted))
            for e in range(CHUNKS):
                for d in SIDES:
                    part_copy(e, d).start()
    for l in range(levels):
        for copy in weights_in[l]:
            copy.start()

    def along(h, i, k):
        return (k, i) if h % 2 else (i, k)

    def place(h, i, k):
        return pool.at[pl.ds(chip_at(*along(h, i, k)) * boxes + chunk * h, chunk)]

    def ring_copy(h, k, sending):
        where = place(h, 0, 0 if sending else 4 - k)
        return pltpu.make_async_remote_copy(
            where, where, ring_ssem.at[h, k - 1], ring_rsem.at[h, k - 1],
            device_id=device_at(*along(h, 0, k)), device_id_type=MESH)

    def cross_copy(h, j, k, sending):
        where = place(h, 0 if sending else 4 - k, j)
        return pltpu.make_async_remote_copy(
            where, where, cross_ssem.at[h, j, k - 1], cross_rsem.at[h, j, k - 1],
            device_id=device_at(*along(h, k, 0)), device_id_type=MESH)

    mine = chip_at(0, 0) * boxes
    for h in range(CHUNKS):
        for d in (1, 3, 2):
            part_copy(h, d).wait_recv()
        total = part_send[tx, pl.ds(chunk * h, chunk)].astype(jnp.float32)
        for d in range(3):
            total = total + part_recv[d, pl.ds(chunk * h, chunk)].astype(jnp.float32)
        pool[pl.ds(mine + chunk * h, chunk)] = total.astype(jnp.bfloat16)
        for k in SIDES:
            ring_copy(h, k, True).start()
        for k in SIDES:
            cross_copy(h, 0, k, True).start()
    for h in range(CHUNKS):
        for k in (1, 3, 2):
            ring_copy(h, k, False).wait_recv()
            for i in SIDES:
                cross_copy(h, 4 - k, i, True).start()
    for h in range(CHUNKS):
        for j in range(4):
            for k in SIDES:
                cross_copy(h, j, k, False).wait_recv()

    def chosen_box(slot):
        box = slots[slot]
        dev = lax.shift_right_logical(box, 4)
        at = lax.shift_right_logical(dev, 1) * boxes + jnp.bitwise_and(box, 15)
        here = jnp.where(jnp.bitwise_and(dev, 1) == core, 1.0, 0.0).astype(jnp.float32)
        return pool[at].astype(jnp.float32) * here

    for s in range(boxes):
        core_send[s] = chosen_box(core_mate[0] * boxes + s).astype(jnp.bfloat16)
    core_copy = pltpu.make_async_remote_copy(
        core_send, core_recv, core_ssem, core_rsem, device_id=core_mate, device_id_type=MESH)
    core_copy.start()
    own = [chosen_box(me * boxes + s) for s in range(boxes)]
    core_copy.wait_recv()
    for s in range(boxes):
        state[0, s] = (own[s] + core_recv[s].astype(jnp.float32)).astype(jnp.bfloat16)

    lanes = lax.broadcasted_iota(jnp.int32, (own_cols, 128), 1)

    def mixed(a, b, w):
        a, b = a.astype(jnp.float32), b.astype(jnp.float32)
        real = jnp.where(lanes < 64, a, pltpu.roll(b, 64, axis=1))
        imag = jnp.where(lanes < 64, pltpu.roll(a, 64, axis=1), b)
        both = jnp.concatenate([real, imag], axis=0).astype(jnp.bfloat16)
        r = jnp.dot(both, w, preferred_element_type=jnp.float32)
        return turned(r, own_cols).astype(jnp.bfloat16)

    def level_copy(l, g):
        part = pl.ds(per * g, per)
        return pltpu.make_async_remote_copy(
            state.at[l, part], partner.at[l - local, part],
            level_ssem.at[l - local, g], level_rsem.at[l - local, g], device_id=mates[l - local], device_id_type=MESH)

    for l in range(levels):
        for copy in weights_in[l]:
            copy.wait()
        for g in range(GROUPS):
            if l >= local:
                level_copy(l, g).wait_recv()
            for s in range(per * g, per * g + per):
                other = state[l, s ^ (1 << l)] if l < local else partner[l - local, s]
                new = mixed(state[l, s], other, weights[l, s])
                if l + 1 < levels:
                    state[l + 1, s] = new
                else:
                    out_ref[s] = new
            if local <= l + 1 < levels:
                level_copy(l + 1, g).start()

    for h in range(CHUNKS):
        for d in (1, 2, 3):
            part_copy(h, d).wait_send()
            ring_copy(h, d, True).wait_send()
            for j in range(4):
                cross_copy(h, j, d, True).wait_send()
    core_copy.wait_send()
    for l in range(local, levels):
        for g in range(GROUPS):
            level_copy(l, g).wait_send()


def coefs_of_device(pick, slot_box, bank, leaf_factor, self_factor, cross_factor):
    boxes = bank.shape[0]
    levels = self_factor.shape[0]
    cols = pick.shape[0] // 4
    crossing = levels - boxes.bit_length() + 1
    bf16 = jnp.bfloat16
    dma = pltpu.SemaphoreType.DMA
    hbm = pl.BlockSpec(memory_space=pltpu.HBM)
    tiles = lambda *lead: pltpu.VMEM((*lead, cols, 128), bf16)
    pair = lambda *shape: [dma(shape), dma(shape)]
    return pl.pallas_call(
        coefs_kernel,
        out_shape=jax.ShapeDtypeStruct((boxes, cols, 128), bf16),
        in_specs=[hbm] * 6,
        out_specs=pl.BlockSpec(memory_space=pltpu.VMEM),
        scratch_shapes=[
            pltpu.SMEM(pick.shape, jnp.int32),
            pltpu.SMEM(slot_box.shape, jnp.int32),
            pltpu.VMEM(bank.shape, bf16),
            pltpu.VMEM(leaf_factor.shape, bf16),
            pltpu.VMEM((levels, boxes, 128, 128), bf16),
            tiles(4, boxes), tiles(3, boxes), tiles(16 * boxes), tiles(boxes), tiles(boxes),
            tiles(levels, boxes), tiles(crossing, boxes),
            dma((2,)), dma((boxes,)), dma((CHUNKS,)), dma((levels, 2)),
            *pair(CHUNKS, 3), *pair(CHUNKS, 3), *pair(CHUNKS, 4, 3), dma, dma, *pair(crossing, GROUPS),
        ],
        compiler_params=pltpu.CompilerParams(
            collective_id=0, has_side_effects=True, vmem_limit_bytes=VMEM_MIB << 20),
        name="coefs",
    )(pick, slot_box, bank, leaf_factor, self_factor, cross_factor)


def target_kernel(x_ref, t_ref, o_ref):
    for s in range(x_ref.shape[0]):
        x = x_ref[s].astype(jnp.float32)
        both = jnp.concatenate([x, pltpu.roll(x, 64, axis=1)], axis=0)[:, :64].astype(jnp.bfloat16)
        rows = x.shape[0]
        half = t_ref.shape[2] // 2
        r = jnp.dot(both, t_ref[s], preferred_element_type=jnp.float32)
        o_ref[s, :, :half] = (r[:rows, :half] - r[rows:, half:]).astype(jnp.bfloat16)
        o_ref[s, :, half:] = (r[:rows, half:] + r[rows:, :half]).astype(jnp.bfloat16)


def target_map(x, target_factor):
    boxes, cols, _ = x.shape
    k, width = target_factor.shape[1:]
    step = 4
    return pl.pallas_call(
        target_kernel,
        out_shape=jax.ShapeDtypeStruct((boxes, cols, width), jnp.bfloat16),
        grid=(boxes // step,),
        in_specs=[
            pl.BlockSpec((step, cols, 128), lambda i: (i, 0, 0)),
            pl.BlockSpec((step, k, width), lambda i: (i, 0, 0)),
        ],
        out_specs=pl.BlockSpec((step, cols, width), lambda i: (i, 0, 0)),
        compiler_params=pltpu.CompilerParams(vmem_limit_bytes=16 << 20),
        name="target_map",
    )(x, target_factor)


def per_device(bank, pick, slot_box, leaf_factor, self_factor, cross_factor, target_factor):
    x = coefs_of_device(pick, slot_box, bank, leaf_factor, self_factor, cross_factor)
    return target_map(x, target_factor)


def solution(mesh):
    in_specs = (
        P("box", "tx", None),
        P(),
        P(),
        P("box", None, None),
        P(None, "box", None, None),
        P(None, "box", None, None),
        P("box", None, None),
    )
    out_specs = P("box", "tx", None)
    return jax.shard_map(
        per_device, mesh=mesh, in_specs=in_specs, out_specs=out_specs, check_vma=False
    )
```

```python
import functools

import jax
import jax.numpy as jnp
from jax import lax
from jax.experimental import pallas as pl
from jax.experimental.pallas import tpu as pltpu
from jax.sharding import PartitionSpec as P

MESH = pl.DeviceIdType.MESH
GROUPS = 4
CHUNKS = 4
VMEM_MIB = 54
SIDES = (2, 1, 3)


def coefs_kernel(
    pick_ref, slot_ref, bank_ref, leaf_ref, self_ref, cross_ref, out_ref,
    picks, slots, bank_buf, leaf_buf, weights, part_send, part_recv, pool, core_send, core_recv,
    state, partner,
    index_sem, bank_sem, leaf_sem, weight_sem, part_ssem, part_rsem, pool_ssem, ring_rsem, cross_rsem,
    core_ssem, core_rsem, level_ssem, level_rsem,
):
    boxes, stored = bank_ref.shape[:2]
    columns = pick_ref.shape[0]
    own_cols = columns // 4
    levels = self_ref.shape[0]
    chunk = boxes // CHUNKS
    per = boxes // GROUPS
    local = boxes.bit_length() - 1
    me = lax.axis_index("box")
    tx = lax.axis_index("tx")
    y = me // 8
    z = (me // 2) % 4
    core = me % 2

    def chip_at(dy, dz):
        return ((y + dy) % 4) * 4 + (z + dz) % 4

    def device_at(dy, dz):
        return ((y + dy) % 4) * 8 + ((z + dz) % 4) * 2 + core, tx

    core_mate = (y * 8 + z * 2 + 1 - core, tx)
    mates = [
        core_mate,
        device_at(0, 1 + 2 * (z % 2)),
        device_at(0, 2),
        device_at(1 + 2 * (y % 2), 0),
        device_at(2, 0),
    ]

    barrier = pltpu.get_barrier_semaphore()
    greeted = ([(me, (tx + d) % 4) for d in SIDES] + [device_at(0, d) for d in SIDES]
               + [device_at(d, 0) for d in SIDES] + [core_mate])
    for dev in greeted:
        pl.semaphore_signal(barrier, inc=1, device_id=dev, device_id_type=MESH)

    index_in = [
        pltpu.make_async_copy(pick_ref, picks, index_sem.at[0]),
        pltpu.make_async_copy(slot_ref, slots, index_sem.at[1]),
    ]
    bank_in, leaf_in = [[
        pltpu.make_async_copy(ref.at[pl.ds(chunk * h, chunk)], buf.at[pl.ds(chunk * h, chunk)], sem.at[h])
        for h in range(CHUNKS)
    ] for ref, buf, sem in ((bank_ref, bank_buf, bank_sem), (leaf_ref, leaf_buf, leaf_sem))]
    weights_in = [
        pltpu.make_async_copy(ref, weights.at[:, :, pl.ds(128 * i, 64), :], weight_sem.at[i])
        for i, ref in enumerate((self_ref, cross_ref))
    ]

    def fetch(h):
        leaf_in[h].start()
        bank_in[h].start()

    for copy in index_in:
        copy.start()
    fetch(0)
    fetch(1)

    for copy in index_in:
        copy.wait()
    lane = lax.broadcasted_iota(jnp.int32, (8, stored), 1)
    row = lax.broadcasted_iota(jnp.int32, (8, stored), 0)
    tiles = []
    for g in range(columns // 8):
        want = jnp.full((8, stored), -1, jnp.int32)
        for i in range(8):
            want = jnp.where(row == i, picks[8 * g + i] - tx * stored, want)
        tiles.append(jnp.where(want == lane, 1.0, 0.0).astype(jnp.float32))
    chooser = jnp.concatenate(tiles, axis=0).astype(jnp.bfloat16)

    def turned(r, rows):
        lanes = lax.broadcasted_iota(jnp.int32, (rows, 128), 1)
        second = pltpu.roll(r[rows:], 64, axis=1)
        return r[:rows] + jnp.where(lanes < 64, -second, second)

    def leaf_of(b):
        chosen = jnp.dot(chooser, bank_buf[b], preferred_element_type=jnp.float32).astype(jnp.bfloat16)
        half = chosen.shape[1] // 2
        both = jnp.concatenate([chosen[:, :half], chosen[:, half:]], axis=0)
        r = jnp.dot(both, leaf_buf[b], preferred_element_type=jnp.float32)
        coefs = turned(r, columns).astype(jnp.bfloat16)
        for t in range(4):
            part_send[t, b] = coefs[t * own_cols:(t + 1) * own_cols]

    def part_copy(h, d):
        to = (tx + d) % 4
        return pltpu.make_async_remote_copy(
            part_send.at[to, pl.ds(chunk * h, chunk)], part_recv.at[d - 1, pl.ds(chunk * h, chunk)],
            part_ssem, part_rsem.at[h],
            device_id=(me, to), device_id_type=MESH)

    for h in range(CHUNKS):
        leaf_in[h].wait()
        bank_in[h].wait()
        if h + 2 < CHUNKS:
            fetch(h + 2)
        else:
            weights_in[h + 2 - CHUNKS].start()
        for b in range(chunk * h, chunk * h + chunk):
            leaf_of(b)
        if h == CHUNKS - 1:
            pl.semaphore_wait(barrier, len(greeted))
            for e in range(CHUNKS):
                for d in SIDES:
                    part_copy(e, d).start()

    for copy in weights_in:
        copy.wait()
    side = lax.broadcasted_iota(jnp.int32, (64, 128), 1) < 64

    def widen(l, s):
        for i in (0, 128):
            m = weights[l, s, i:i + 64].astype(jnp.float32)
            m = pltpu.roll(m, 64, axis=1)
            weights[l, s, i + 64:i + 128] = jnp.where(side, -m, m).astype(jnp.bfloat16)

    def widen_level(l, carry):
        def some(i, carry):
            for s in range(4):
                widen(l, 4 * i + s)
            return carry
        return lax.fori_loop(0, boxes // 4, some, carry)

    lax.fori_loop(0, local, widen_level, 0)

    def along(h, i, k):
        return (k, i) if h % 2 else (i, k)

    def place(h, i, k):
        return pool.at[pl.ds(chip_at(*along(h, i, k)) * boxes + chunk * h, chunk)]

    def ring_copy(h, k, sending):
        where = place(h, 0, 0 if sending else 4 - k)
        return pltpu.make_async_remote_copy(
            where, where, pool_ssem, ring_rsem.at[h, k - 1],
            device_id=device_at(*along(h, 0, k)), device_id_type=MESH)

    def cross_copy(h, j, k, sending):
        where = place(h, 0 if sending else 4 - k, j)
        return pltpu.make_async_remote_copy(
            where, where, pool_ssem, cross_rsem,
            device_id=device_at(*along(h, k, 0)), device_id_type=MESH)

    mine = chip_at(0, 0) * boxes
    for h in range(CHUNKS):
        whole = part_recv.at[:, pl.ds(chunk * h, chunk)]
        pltpu.make_async_copy(whole, whole, part_rsem.at[h]).wait()
        total = part_send[tx, pl.ds(chunk * h, chunk)].astype(jnp.float32)
        for d in range(3):
            total = total + part_recv[d, pl.ds(chunk * h, chunk)].astype(jnp.float32)
        pool[pl.ds(mine + chunk * h, chunk)] = total.astype(jnp.bfloat16)
        for k in SIDES:
            ring_copy(h, k, True).start()
        if h % 2:
            for e in (h - 1, h):
                for k in SIDES:
                    cross_copy(e, 0, k, True).start()
    for h in range(CHUNKS):
        for k in (1, 3, 2):
            ring_copy(h, k, False).wait_recv()
            for i in SIDES:
                cross_copy(h, 4 - k, i, True).start()
    lax.fori_loop(local, levels, widen_level, 0)
    crossed = pool.at[pl.ds(0, 12 * boxes)]
    pltpu.make_async_copy(crossed, crossed, cross_rsem).wait()

    def chosen_box(slot):
        box = slots[slot]
        dev = lax.shift_right_logical(box, 4)
        at = lax.shift_right_logical(dev, 1) * boxes + jnp.bitwise_and(box, 15)
        here = jnp.where(jnp.bitwise_and(dev, 1) == core, 1.0, 0.0).astype(jnp.float32)
        return pool[at].astype(jnp.float32) * here

    for s in range(boxes):
        core_send[s] = chosen_box(core_mate[0] * boxes + s).astype(jnp.bfloat16)
    core_copy = pltpu.make_async_remote_copy(
        core_send, core_recv, core_ssem, core_rsem, device_id=core_mate, device_id_type=MESH)
    core_copy.start()
    own = [chosen_box(me * boxes + s) for s in range(boxes)]
    core_copy.wait_recv()
    for s in range(boxes):
        state[0, s] = (own[s] + core_recv[s].astype(jnp.float32)).astype(jnp.bfloat16)

    def level_copy(l, g):
        part = pl.ds(per * g, per)
        return pltpu.make_async_remote_copy(
            state.at[l, part], partner.at[l - local, part],
            level_ssem, level_rsem.at[l - local, g], device_id=mates[l - local], device_id_type=MESH)

    def product(x, l, s, i):
        return jnp.dot(x, weights[l, s, i:i + 128], preferred_element_type=jnp.float32)

    for l in range(levels):
        mine_part = [product(state[l, s], l, s, 0) for s in range(boxes)]
        for g in range(GROUPS):
            if l >= local:
                level_copy(l, g).wait_recv()
            for s in range(per * g, per * g + per):
                other = state[l, s ^ (1 << l)] if l < local else partner[l - local, s]
                new = (mine_part[s] + product(other, l, s, 128)).astype(jnp.bfloat16)
                if l + 1 < levels:
                    state[l + 1, s] = new
                else:
                    out_ref[s] = new
            if local <= l + 1 < levels:
                level_copy(l + 1, g).start()

    pltpu.make_async_copy(part_recv, part_recv, part_ssem).wait()
    sent = pool.at[pl.ds(0, 15 * boxes)]
    pltpu.make_async_copy(sent, sent, pool_ssem).wait()
    core_copy.wait_send()
    pltpu.make_async_copy(partner, partner, level_ssem).wait()


def coefs_of_device(pick, slot_box, bank, leaf_factor, self_factor, cross_factor):
    boxes = bank.shape[0]
    levels = self_factor.shape[0]
    cols = pick.shape[0] // 4
    crossing = levels - boxes.bit_length() + 1
    bf16 = jnp.bfloat16
    dma = pltpu.SemaphoreType.DMA
    hbm = pl.BlockSpec(memory_space=pltpu.HBM)
    tiles = lambda *lead: pltpu.VMEM((*lead, cols, 128), bf16)
    return pl.pallas_call(
        coefs_kernel,
        out_shape=jax.ShapeDtypeStruct((boxes, cols, 128), bf16),
        in_specs=[hbm] * 6,
        out_specs=pl.BlockSpec(memory_space=pltpu.VMEM),
        scratch_shapes=[
            pltpu.SMEM(pick.shape, jnp.int32),
            pltpu.SMEM(slot_box.shape, jnp.int32),
            pltpu.VMEM(bank.shape, bf16),
            pltpu.VMEM(leaf_factor.shape, bf16),
            pltpu.VMEM((levels, boxes, 256, 128), bf16),
            tiles(4, boxes), tiles(3, boxes), tiles(16 * boxes), tiles(boxes), tiles(boxes),
            tiles(levels, boxes), tiles(crossing, boxes),
            dma((2,)), dma((CHUNKS,)), dma((CHUNKS,)), dma((2,)),
            dma, dma((CHUNKS,)), dma, dma((CHUNKS, 3)), dma, dma, dma, dma, dma((crossing, GROUPS)),
        ],
        compiler_params=pltpu.CompilerParams(
            collective_id=0, has_side_effects=True, vmem_limit_bytes=VMEM_MIB << 20),
        name="coefs",
    )(pick, slot_box, bank, leaf_factor, self_factor, cross_factor)


def target_kernel(x_ref, t_ref, o_ref):
    for s in range(x_ref.shape[0]):
        x = x_ref[s].astype(jnp.float32)
        both = jnp.concatenate([x, pltpu.roll(x, 64, axis=1)], axis=0)[:, :64].astype(jnp.bfloat16)
        rows = x.shape[0]
        half = t_ref.shape[2] // 2
        r = jnp.dot(both, t_ref[s], preferred_element_type=jnp.float32)
        o_ref[s, :, :half] = (r[:rows, :half] - r[rows:, half:]).astype(jnp.bfloat16)
        o_ref[s, :, half:] = (r[:rows, half:] + r[rows:, :half]).astype(jnp.bfloat16)


def target_map(x, target_factor):
    boxes, cols, _ = x.shape
    k, width = target_factor.shape[1:]
    step = 4
    return pl.pallas_call(
        target_kernel,
        out_shape=jax.ShapeDtypeStruct((boxes, cols, width), jnp.bfloat16),
        grid=(boxes // step,),
        in_specs=[
            pl.BlockSpec((step, cols, 128), lambda i: (i, 0, 0)),
            pl.BlockSpec((step, k, width), lambda i: (i, 0, 0)),
        ],
        out_specs=pl.BlockSpec((step, cols, width), lambda i: (i, 0, 0)),
        compiler_params=pltpu.CompilerParams(vmem_limit_bytes=16 << 20),
        name="target_map",
    )(x, target_factor)


def per_device(bank, pick, slot_box, leaf_factor, self_factor, cross_factor, target_factor):
    x = coefs_of_device(pick, slot_box, bank, leaf_factor, self_factor, cross_factor)
    return target_map(x, target_factor)


def solution(mesh):
    in_specs = (
        P("box", "tx", None),
        P(),
        P(),
        P("box", None, None),
        P(None, "box", None, None),
        P(None, "box", None, None),
        P("box", None, None),
    )
    out_specs = P("box", "tx", None)
    return jax.shard_map(
        per_device, mesh=mesh, in_specs=in_specs, out_specs=out_specs, check_vma=False
    )
```

```python
import functools

import jax
import jax.numpy as jnp
from jax import lax
from jax.experimental import pallas as pl
from jax.experimental.pallas import tpu as pltpu
from jax.sharding import PartitionSpec as P

MESH = pl.DeviceIdType.MESH
GROUPS = 4
CHUNKS = 4
VMEM_MIB = 54
SIDES = (2, 1, 3)


def coefs_kernel(
    pick_ref, slot_ref, bank_ref, leaf_ref, self_ref, cross_ref, out_ref,
    picks, slots, bank_buf, leaf_buf, weights, part_send, part_recv, pool, core_send, core_recv,
    state, partner,
    index_sem, bank_sem, leaf_sem, weight_sem, part_ssem, part_rsem, pool_ssem, ring_rsem, cross_rsem,
    core_ssem, core_rsem, level_ssem, level_rsem,
):
    boxes, stored = bank_ref.shape[:2]
    columns = pick_ref.shape[0]
    own_cols = columns // 4
    levels = self_ref.shape[0]
    chunk = boxes // CHUNKS
    per = boxes // GROUPS
    local = boxes.bit_length() - 1
    me = lax.axis_index("box")
    tx = lax.axis_index("tx")
    y = me // 8
    z = (me // 2) % 4
    core = me % 2

    def chip_at(dy, dz):
        return ((y + dy) % 4) * 4 + (z + dz) % 4

    def device_at(dy, dz):
        return ((y + dy) % 4) * 8 + ((z + dz) % 4) * 2 + core, tx

    core_mate = (y * 8 + z * 2 + 1 - core, tx)
    mates = [
        core_mate,
        device_at(0, 1 + 2 * (z % 2)),
        device_at(0, 2),
        device_at(1 + 2 * (y % 2), 0),
        device_at(2, 0),
    ]

    barrier = pltpu.get_barrier_semaphore()
    greeted = ([(me, (tx + d) % 4) for d in SIDES] + [device_at(0, d) for d in SIDES]
               + [device_at(d, 0) for d in SIDES] + [core_mate])
    for dev in greeted:
        pl.semaphore_signal(barrier, inc=1, device_id=dev, device_id_type=MESH)

    index_in = [
        pltpu.make_async_copy(pick_ref, picks, index_sem.at[0]),
        pltpu.make_async_copy(slot_ref, slots, index_sem.at[1]),
    ]
    bank_in, leaf_in = [[
        pltpu.make_async_copy(ref.at[pl.ds(chunk * h, chunk)], buf.at[pl.ds(chunk * h, chunk)], sem.at[h])
        for h in range(CHUNKS)
    ] for ref, buf, sem in ((bank_ref, bank_buf, bank_sem), (leaf_ref, leaf_buf, leaf_sem))]
    weights_in = [
        pltpu.make_async_copy(ref, weights.at[:, :, pl.ds(128 * i, 64), :], weight_sem.at[i])
        for i, ref in enumerate((self_ref, cross_ref))
    ]

    def fetch(h):
        leaf_in[h].start()
        bank_in[h].start()

    for copy in index_in:
        copy.start()
    fetch(0)
    fetch(1)

    for copy in index_in:
        copy.wait()
    lane = lax.broadcasted_iota(jnp.int32, (8, stored), 1)
    row = lax.broadcasted_iota(jnp.int32, (8, stored), 0)
    tiles = []
    for g in range(columns // 8):
        want = jnp.full((8, stored), -1, jnp.int32)
        for i in range(8):
            want = jnp.where(row == i, picks[8 * g + i] - tx * stored, want)
        tiles.append(jnp.where(want == lane, 1.0, 0.0).astype(jnp.float32))
    chooser = jnp.concatenate(tiles, axis=0).astype(jnp.bfloat16)

    def turned(r, rows):
        lanes = lax.broadcasted_iota(jnp.int32, (rows, 128), 1)
        second = pltpu.roll(r[rows:], 64, axis=1)
        return r[:rows] + jnp.where(lanes < 64, -second, second)

    def leaf_of(b):
        chosen = jnp.dot(chooser, bank_buf[b], preferred_element_type=jnp.float32).astype(jnp.bfloat16)
        half = chosen.shape[1] // 2
        both = jnp.concatenate([chosen[:, :half], chosen[:, half:]], axis=0)
        r = jnp.dot(both, leaf_buf[b], preferred_element_type=jnp.float32)
        coefs = turned(r, columns).astype(jnp.bfloat16)
        for t in range(4):
            part_send[t, b] = coefs[t * own_cols:(t + 1) * own_cols]

    def part_copy(h, d):
        to = (tx + d) % 4
        return pltpu.make_async_remote_copy(
            part_send.at[to, pl.ds(chunk * h, chunk)], part_recv.at[d - 1, pl.ds(chunk * h, chunk)],
            part_ssem, part_rsem.at[h],
            device_id=(me, to), device_id_type=MESH)

    for h in range(CHUNKS):
        leaf_in[h].wait()
        bank_in[h].wait()
        if h + 2 < CHUNKS:
            fetch(h + 2)
        else:
            weights_in[h + 2 - CHUNKS].start()
        for b in range(chunk * h, chunk * h + chunk):
            leaf_of(b)
        if h == 1:
            pl.semaphore_wait(barrier, len(greeted))
        for e in range(h + 1) if h == 1 else [h] if h > 1 else []:
            for d in SIDES:
                part_copy(e, d).start()

    for copy in weights_in:
        copy.wait()
    side = lax.broadcasted_iota(jnp.int32, (64, 128), 1) < 64

    def widen(l, s):
        for i in (0, 128):
            m = weights[l, s, i:i + 64].astype(jnp.float32)
            m = pltpu.roll(m, 64, axis=1)
            weights[l, s, i + 64:i + 128] = jnp.where(side, -m, m).astype(jnp.bfloat16)

    def widen_level(l, carry):
        def some(i, carry):
            for s in range(4):
                widen(l, 4 * i + s)
            return carry
        return lax.fori_loop(0, boxes // 4, some, carry)

    lax.fori_loop(0, local, widen_level, 0)

    def along(h, i, k):
        return (k, i) if h % 2 else (i, k)

    def place(h, i, k):
        return pool.at[pl.ds(chip_at(*along(h, i, k)) * boxes + chunk * h, chunk)]

    def ring_copy(h, k, sending):
        where = place(h, 0, 0 if sending else 4 - k)
        return pltpu.make_async_remote_copy(
            where, where, pool_ssem, ring_rsem.at[h, k - 1],
            device_id=device_at(*along(h, 0, k)), device_id_type=MESH)

    def cross_copy(h, j, k, sending):
        where = place(h, 0 if sending else 4 - k, j)
        return pltpu.make_async_remote_copy(
            where, where, pool_ssem, cross_rsem,
            device_id=device_at(*along(h, k, 0)), device_id_type=MESH)

    mine = chip_at(0, 0) * boxes
    for h in range(CHUNKS):
        whole = part_recv.at[:, pl.ds(chunk * h, chunk)]
        pltpu.make_async_copy(whole, whole, part_rsem.at[h]).wait()
        total = part_send[tx, pl.ds(chunk * h, chunk)].astype(jnp.float32)
        for d in range(3):
            total = total + part_recv[d, pl.ds(chunk * h, chunk)].astype(jnp.float32)
        pool[pl.ds(mine + chunk * h, chunk)] = total.astype(jnp.bfloat16)
        for k in SIDES:
            ring_copy(h, k, True).start()
        for k in SIDES:
            cross_copy(h, 0, k, True).start()
    for h in range(CHUNKS):
        for k in (1, 3, 2):
            ring_copy(h, k, False).wait_recv()
            for i in SIDES:
                cross_copy(h, 4 - k, i, True).start()
    lax.fori_loop(local, levels, widen_level, 0)
    crossed = pool.at[pl.ds(0, 12 * boxes)]
    pltpu.make_async_copy(crossed, crossed, cross_rsem).wait()

    def chosen_box(slot):
        box = slots[slot]
        dev = lax.shift_right_logical(box, 4)
        at = lax.shift_right_logical(dev, 1) * boxes + jnp.bitwise_and(box, 15)
        here = jnp.where(jnp.bitwise_and(dev, 1) == core, 1.0, 0.0).astype(jnp.float32)
        return pool[at].astype(jnp.float32) * here

    for s in range(boxes):
        core_send[s] = chosen_box(core_mate[0] * boxes + s).astype(jnp.bfloat16)
    core_copy = pltpu.make_async_remote_copy(
        core_send, core_recv, core_ssem, core_rsem, device_id=core_mate, device_id_type=MESH)
    core_copy.start()
    own = [chosen_box(me * boxes + s) for s in range(boxes)]
    core_copy.wait_recv()
    for s in range(boxes):
        state[0, s] = (own[s] + core_recv[s].astype(jnp.float32)).astype(jnp.bfloat16)

    def level_copy(l, g):
        part = pl.ds(per * g, per)
        return pltpu.make_async_remote_copy(
            state.at[l, part], partner.at[l - local, part],
            level_ssem, level_rsem.at[l - local, g], device_id=mates[l - local], device_id_type=MESH)

    def product(x, l, s, i):
        return jnp.dot(x, weights[l, s, i:i + 128], preferred_element_type=jnp.float32)

    for l in range(levels):
        mine_part = [product(state[l, s], l, s, 0) for s in range(boxes)]
        for g in range(GROUPS):
            if l >= local:
                level_copy(l, g).wait_recv()
            for s in range(per * g, per * g + per):
                other = state[l, s ^ (1 << l)] if l < local else partner[l - local, s]
                new = (mine_part[s] + product(other, l, s, 128)).astype(jnp.bfloat16)
                if l + 1 < levels:
                    state[l + 1, s] = new
                else:
                    out_ref[s] = new
            if local <= l + 1 < levels:
                level_copy(l + 1, g).start()

    pltpu.make_async_copy(part_recv, part_recv, part_ssem).wait()
    sent = pool.at[pl.ds(0, 15 * boxes)]
    pltpu.make_async_copy(sent, sent, pool_ssem).wait()
    core_copy.wait_send()
    pltpu.make_async_copy(partner, partner, level_ssem).wait()


def coefs_of_device(pick, slot_box, bank, leaf_factor, self_factor, cross_factor):
    boxes = bank.shape[0]
    levels = self_factor.shape[0]
    cols = pick.shape[0] // 4
    crossing = levels - boxes.bit_length() + 1
    bf16 = jnp.bfloat16
    dma = pltpu.SemaphoreType.DMA
    hbm = pl.BlockSpec(memory_space=pltpu.HBM)
    tiles = lambda *lead: pltpu.VMEM((*lead, cols, 128), bf16)
    return pl.pallas_call(
        coefs_kernel,
        out_shape=jax.ShapeDtypeStruct((boxes, cols, 128), bf16),
        in_specs=[hbm] * 6,
        out_specs=pl.BlockSpec(memory_space=pltpu.VMEM),
        scratch_shapes=[
            pltpu.SMEM(pick.shape, jnp.int32),
            pltpu.SMEM(slot_box.shape, jnp.int32),
            pltpu.VMEM(bank.shape, bf16),
            pltpu.VMEM(leaf_factor.shape, bf16),
            pltpu.VMEM((levels, boxes, 256, 128), bf16),
            tiles(4, boxes), tiles(3, boxes), tiles(16 * boxes), tiles(boxes), tiles(boxes),
            tiles(levels, boxes), tiles(crossing, boxes),
            dma((2,)), dma((CHUNKS,)), dma((CHUNKS,)), dma((2,)),
            dma, dma((CHUNKS,)), dma, dma((CHUNKS, 3)), dma, dma, dma, dma, dma((crossing, GROUPS)),
        ],
        compiler_params=pltpu.CompilerParams(
            collective_id=0, has_side_effects=True, vmem_limit_bytes=VMEM_MIB << 20),
        name="coefs",
    )(pick, slot_box, bank, leaf_factor, self_factor, cross_factor)


def target_kernel(x_ref, t_ref, o_ref, buf, sem):
    boxes, cols, _ = x_ref.shape
    width = o_ref.shape[2] // 2
    tile = 256
    first = lax.broadcasted_iota(jnp.int32, (cols, 128), 1) < 64
    copies = [
        pltpu.make_async_copy(buf.at[pl.ds(4 * g, 4)], o_ref.at[pl.ds(4 * g, 4)], sem.at[g])
        for g in range(boxes // 4)
    ]
    for g in range(boxes // 4):
        rows = []
        for i in range(4):
            x = x_ref[4 * g + i].astype(jnp.float32)
            swapped = pltpu.roll(x, 64, axis=1)
            if i % 2 == 0:
                pairs = [jnp.where(first, x, 0.0), jnp.where(first, swapped, 0.0)]
            else:
                pairs = [jnp.where(first, 0.0, swapped), jnp.where(first, 0.0, x)]
            block = jnp.concatenate(pairs, axis=0)
            none = jnp.zeros_like(block)
            rows.append(jnp.concatenate([block, none] if i < 2 else [none, block], axis=1))
        left = jnp.concatenate(rows, axis=0).astype(jnp.bfloat16)
        part = slice(256 * g, 256 * g + 256)
        for c in range(0, width, tile):
            re, im = [
                jnp.dot(left, t_ref[part, at:at + tile], preferred_element_type=jnp.float32)
                for at in (c, width + c)
            ]
            for i in range(4):
                a, b, e = 2 * cols * i, 2 * cols * i + cols, 2 * cols * i + 2 * cols
                buf[4 * g + i, :, c:c + tile] = (re[a:b] - im[b:e]).astype(jnp.bfloat16)
                buf[4 * g + i, :, width + c:width + c + tile] = (im[a:b] + re[b:e]).astype(jnp.bfloat16)
        copies[g].start()
    for copy in copies:
        copy.wait()


def target_map(x, target_factor):
    boxes, cols, _ = x.shape
    k, width = target_factor.shape[1:]
    vmem = pl.BlockSpec(memory_space=pltpu.VMEM)
    return pl.pallas_call(
        target_kernel,
        out_shape=jax.ShapeDtypeStruct((boxes, cols, width), jnp.bfloat16),
        in_specs=[vmem, vmem],
        out_specs=pl.BlockSpec(memory_space=pltpu.HBM),
        scratch_shapes=[pltpu.VMEM((boxes, cols, width), jnp.bfloat16), pltpu.SemaphoreType.DMA((boxes // 4,))],
        compiler_params=pltpu.CompilerParams(vmem_limit_bytes=16 << 20),
        name="target_map",
    )(x, target_factor.reshape(boxes * k, width))


def per_device(bank, pick, slot_box, leaf_factor, self_factor, cross_factor, target_factor):
    x = coefs_of_device(pick, slot_box, bank, leaf_factor, self_factor, cross_factor)
    return target_map(x, target_factor)


def solution(mesh):
    in_specs = (
        P("box", "tx", None),
        P(),
        P(),
        P("box", None, None),
        P(None, "box", None, None),
        P(None, "box", None, None),
        P("box", None, None),
    )
    out_specs = P("box", "tx", None)
    return jax.shard_map(
        per_device, mesh=mesh, in_specs=in_specs, out_specs=out_specs, check_vma=False
    )
```

```python
import functools

import jax
import jax.numpy as jnp
from jax import lax
from jax.experimental import pallas as pl
from jax.experimental.pallas import tpu as pltpu
from jax.sharding import PartitionSpec as P

MESH = pl.DeviceIdType.MESH
GROUPS = 4
CHUNKS = 4
VMEM_MIB = 54
SIDES = (2, 1, 3)


def coefs_kernel(
    pick_ref, slot_ref, bank_ref, leaf_ref, self_ref, cross_ref, out_ref,
    picks, slots, bank_buf, leaf_buf, weights, part_send, part_recv, pool, core_send, core_recv,
    state, partner,
    index_sem, bank_sem, leaf_sem, weight_sem, part_ssem, part_rsem, pool_ssem, ring_rsem, cross_rsem,
    core_ssem, core_rsem, level_ssem, level_rsem,
):
    boxes, stored = bank_ref.shape[:2]
    columns = pick_ref.shape[0]
    own_cols = columns // 4
    levels = self_ref.shape[0]
    chunk = boxes // CHUNKS
    per = boxes // GROUPS
    local = boxes.bit_length() - 1
    me = lax.axis_index("box")
    tx = lax.axis_index("tx")
    y = me // 8
    z = (me // 2) % 4
    core = me % 2

    def chip_at(dy, dz):
        return ((y + dy) % 4) * 4 + (z + dz) % 4

    def device_at(dy, dz):
        return ((y + dy) % 4) * 8 + ((z + dz) % 4) * 2 + core, tx

    core_mate = (y * 8 + z * 2 + 1 - core, tx)
    mates = [
        core_mate,
        device_at(0, 1 + 2 * (z % 2)),
        device_at(0, 2),
        device_at(1 + 2 * (y % 2), 0),
        device_at(2, 0),
    ]

    barrier = pltpu.get_barrier_semaphore()
    greeted = ([(me, (tx + d) % 4) for d in SIDES] + [device_at(0, d) for d in SIDES]
               + [device_at(d, 0) for d in SIDES] + [core_mate])
    for dev in greeted:
        pl.semaphore_signal(barrier, inc=1, device_id=dev, device_id_type=MESH)

    index_in = [
        pltpu.make_async_copy(pick_ref, picks, index_sem.at[0]),
        pltpu.make_async_copy(slot_ref, slots, index_sem.at[1]),
    ]
    bank_in, leaf_in = [[
        pltpu.make_async_copy(ref.at[pl.ds(chunk * h, chunk)], buf.at[pl.ds(chunk * h, chunk)], sem.at[h])
        for h in range(CHUNKS)
    ] for ref, buf, sem in ((bank_ref, bank_buf, bank_sem), (leaf_ref, leaf_buf, leaf_sem))]
    weights_in = [
        pltpu.make_async_copy(ref, weights.at[:, :, pl.ds(128 * i, 64), :], weight_sem.at[i])
        for i, ref in enumerate((self_ref, cross_ref))
    ]

    def fetch(h):
        leaf_in[h].start()
        bank_in[h].start()

    for copy in index_in:
        copy.start()
    fetch(0)
    fetch(1)
    fetch(2)

    for copy in index_in:
        copy.wait()
    lane = lax.broadcasted_iota(jnp.int32, (8, stored), 1)
    row = lax.broadcasted_iota(jnp.int32, (8, stored), 0)
    tiles = []
    for g in range(columns // 8):
        want = jnp.full((8, stored), -1, jnp.int32)
        for i in range(8):
            want = jnp.where(row == i, picks[8 * g + i] - tx * stored, want)
        tiles.append(jnp.where(want == lane, 1.0, 0.0).astype(jnp.float32))
    chooser = jnp.concatenate(tiles, axis=0).astype(jnp.bfloat16)

    def turned(r, rows):
        lanes = lax.broadcasted_iota(jnp.int32, (rows, 128), 1)
        second = pltpu.roll(r[rows:], 64, axis=1)
        return r[:rows] + jnp.where(lanes < 64, -second, second)

    def leaf_of(b):
        chosen = jnp.dot(chooser, bank_buf[b], preferred_element_type=jnp.float32).astype(jnp.bfloat16)
        half = chosen.shape[1] // 2
        both = jnp.concatenate([chosen[:, :half], chosen[:, half:]], axis=0)
        r = jnp.dot(both, leaf_buf[b], preferred_element_type=jnp.float32)
        coefs = turned(r, columns).astype(jnp.bfloat16)
        for t in range(4):
            part_send[t, b] = coefs[t * own_cols:(t + 1) * own_cols]

    def part_copy(h, d):
        to = (tx + d) % 4
        return pltpu.make_async_remote_copy(
            part_send.at[to, pl.ds(chunk * h, chunk)], part_recv.at[d - 1, pl.ds(chunk * h, chunk)],
            part_ssem, part_rsem.at[h],
            device_id=(me, to), device_id_type=MESH)

    for h in range(CHUNKS):
        leaf_in[h].wait()
        bank_in[h].wait()
        if h + 3 < CHUNKS:
            fetch(h + 3)
        elif h >= CHUNKS - 2:
            weights_in[h + 2 - CHUNKS].start()
        for b in range(chunk * h, chunk * h + chunk):
            leaf_of(b)
        if h == 1:
            pl.semaphore_wait(barrier, len(greeted))
        for e in range(h + 1) if h == 1 else [h] if h > 1 else []:
            for d in SIDES:
                part_copy(e, d).start()

    side = lax.broadcasted_iota(jnp.int32, (64, 128), 1) < 64

    def widen(l, s):
        for i in (0, 128):
            m = weights[l, s, i:i + 64].astype(jnp.float32)
            m = pltpu.roll(m, 64, axis=1)
            weights[l, s, i + 64:i + 128] = jnp.where(side, -m, m).astype(jnp.bfloat16)

    def widen_level(l, carry):
        def some(i, carry):
            for s in range(4):
                widen(l, 4 * i + s)
            return carry
        return lax.fori_loop(0, boxes // 4, some, carry)

    def along(h, i, k):
        return (k, i) if h % 2 else (i, k)

    def place(h, i, k):
        return pool.at[pl.ds(chip_at(*along(h, i, k)) * boxes + chunk * h, chunk)]

    def ring_copy(h, k, sending):
        where = place(h, 0, 0 if sending else 4 - k)
        return pltpu.make_async_remote_copy(
            where, where, pool_ssem, ring_rsem.at[h, k - 1],
            device_id=device_at(*along(h, 0, k)), device_id_type=MESH)

    def cross_copy(h, j, k, sending):
        where = place(h, 0 if sending else 4 - k, j)
        return pltpu.make_async_remote_copy(
            where, where, pool_ssem, cross_rsem,
            device_id=device_at(*along(h, k, 0)), device_id_type=MESH)

    mine = chip_at(0, 0) * boxes
    for h in range(CHUNKS):
        whole = part_recv.at[:, pl.ds(chunk * h, chunk)]
        pltpu.make_async_copy(whole, whole, part_rsem.at[h]).wait()
        total = part_send[tx, pl.ds(chunk * h, chunk)].astype(jnp.float32)
        for d in range(3):
            total = total + part_recv[d, pl.ds(chunk * h, chunk)].astype(jnp.float32)
        pool[pl.ds(mine + chunk * h, chunk)] = total.astype(jnp.bfloat16)
        for k in SIDES:
            ring_copy(h, k, True).start()
        for k in SIDES:
            cross_copy(h, 0, k, True).start()
    for h in range(CHUNKS):
        for k in (1, 3, 2):
            ring_copy(h, k, False).wait_recv()
            for i in SIDES:
                cross_copy(h, 4 - k, i, True).start()
    for copy in weights_in:
        copy.wait()
    lax.fori_loop(0, levels, widen_level, 0)
    crossed = pool.at[pl.ds(0, 12 * boxes)]
    pltpu.make_async_copy(crossed, crossed, cross_rsem).wait()

    def chosen_box(slot):
        box = slots[slot]
        dev = lax.shift_right_logical(box, 4)
        at = lax.shift_right_logical(dev, 1) * boxes + jnp.bitwise_and(box, 15)
        here = jnp.where(jnp.bitwise_and(dev, 1) == core, 1.0, 0.0).astype(jnp.float32)
        return pool[at].astype(jnp.float32) * here

    for s in range(boxes):
        core_send[s] = chosen_box(core_mate[0] * boxes + s).astype(jnp.bfloat16)
    core_copy = pltpu.make_async_remote_copy(
        core_send, core_recv, core_ssem, core_rsem, device_id=core_mate, device_id_type=MESH)
    core_copy.start()
    own = [chosen_box(me * boxes + s) for s in range(boxes)]
    core_copy.wait_recv()
    for s in range(boxes):
        state[0, s] = (own[s] + core_recv[s].astype(jnp.float32)).astype(jnp.bfloat16)

    def level_copy(l, g):
        part = pl.ds(per * g, per)
        return pltpu.make_async_remote_copy(
            state.at[l, part], partner.at[l - local, part],
            level_ssem, level_rsem.at[l - local, g], device_id=mates[l - local], device_id_type=MESH)

    def product(x, l, s, i):
        return jnp.dot(x, weights[l, s, i:i + 128], preferred_element_type=jnp.float32)

    for l in range(levels):
        mine_part = [product(state[l, s], l, s, 0) for s in range(boxes)]
        for g in range(GROUPS):
            if l >= local:
                level_copy(l, g).wait_recv()
            for s in range(per * g, per * g + per):
                other = state[l, s ^ (1 << l)] if l < local else partner[l - local, s]
                new = (mine_part[s] + product(other, l, s, 128)).astype(jnp.bfloat16)
                if l + 1 < levels:
                    state[l + 1, s] = new
                else:
                    out_ref[s] = new
            if local <= l + 1 < levels:
                level_copy(l + 1, g).start()

    pltpu.make_async_copy(part_recv, part_recv, part_ssem).wait()
    sent = pool.at[pl.ds(0, 15 * boxes)]
    pltpu.make_async_copy(sent, sent, pool_ssem).wait()
    core_copy.wait_send()
    pltpu.make_async_copy(partner, partner, level_ssem).wait()


def coefs_of_device(pick, slot_box, bank, leaf_factor, self_factor, cross_factor):
    boxes = bank.shape[0]
    levels = self_factor.shape[0]
    cols = pick.shape[0] // 4
    crossing = levels - boxes.bit_length() + 1
    bf16 = jnp.bfloat16
    dma = pltpu.SemaphoreType.DMA
    hbm = pl.BlockSpec(memory_space=pltpu.HBM)
    tiles = lambda *lead: pltpu.VMEM((*lead, cols, 128), bf16)
    return pl.pallas_call(
        coefs_kernel,
        out_shape=jax.ShapeDtypeStruct((boxes, cols, 128), bf16),
        in_specs=[hbm] * 6,
        out_specs=pl.BlockSpec(memory_space=pltpu.VMEM),
        scratch_shapes=[
            pltpu.SMEM(pick.shape, jnp.int32),
            pltpu.SMEM(slot_box.shape, jnp.int32),
            pltpu.VMEM(bank.shape, bf16),
            pltpu.VMEM(leaf_factor.shape, bf16),
            pltpu.VMEM((levels, boxes, 256, 128), bf16),
            tiles(4, boxes), tiles(3, boxes), tiles(16 * boxes), tiles(boxes), tiles(boxes),
            tiles(levels, boxes), tiles(crossing, boxes),
            dma((2,)), dma((CHUNKS,)), dma((CHUNKS,)), dma((2,)),
            dma, dma((CHUNKS,)), dma, dma((CHUNKS, 3)), dma, dma, dma, dma, dma((crossing, GROUPS)),
        ],
        compiler_params=pltpu.CompilerParams(
            collective_id=0, has_side_effects=True, vmem_limit_bytes=VMEM_MIB << 20),
        name="coefs",
    )(pick, slot_box, bank, leaf_factor, self_factor, cross_factor)


def target_kernel(x_ref, t_ref, o_ref, buf, sem):
    boxes, cols, _ = x_ref.shape
    width = o_ref.shape[2] // 2
    tile = 256
    first = lax.broadcasted_iota(jnp.int32, (cols, 128), 1) < 64
    copies = [
        pltpu.make_async_copy(buf.at[pl.ds(4 * g, 4)], o_ref.at[pl.ds(4 * g, 4)], sem.at[g])
        for g in range(boxes // 4)
    ]
    for g in range(boxes // 4):
        rows = []
        for i in range(4):
            x = x_ref[4 * g + i].astype(jnp.float32)
            swapped = pltpu.roll(x, 64, axis=1)
            if i % 2 == 0:
                pairs = [jnp.where(first, x, 0.0), jnp.where(first, swapped, 0.0)]
            else:
                pairs = [jnp.where(first, 0.0, swapped), jnp.where(first, 0.0, x)]
            block = jnp.concatenate(pairs, axis=0)
            none = jnp.zeros_like(block)
            rows.append(jnp.concatenate([block, none] if i < 2 else [none, block], axis=1))
        left = jnp.concatenate(rows, axis=0).astype(jnp.bfloat16)
        part = slice(256 * g, 256 * g + 256)
        for c in range(0, width, tile):
            re, im = [
                jnp.dot(left, t_ref[part, at:at + tile], preferred_element_type=jnp.float32)
                for at in (c, width + c)
            ]
            for i in range(4):
                a, b, e = 2 * cols * i, 2 * cols * i + cols, 2 * cols * i + 2 * cols
                buf[4 * g + i, :, c:c + tile] = (re[a:b] - im[b:e]).astype(jnp.bfloat16)
                buf[4 * g + i, :, width + c:width + c + tile] = (im[a:b] + re[b:e]).astype(jnp.bfloat16)
        copies[g].start()
    for copy in copies:
        copy.wait()


def target_map(x, target_factor):
    boxes, cols, _ = x.shape
    k, width = target_factor.shape[1:]
    vmem = pl.BlockSpec(memory_space=pltpu.VMEM)
    return pl.pallas_call(
        target_kernel,
        out_shape=jax.ShapeDtypeStruct((boxes, cols, width), jnp.bfloat16),
        in_specs=[vmem, vmem],
        out_specs=pl.BlockSpec(memory_space=pltpu.HBM),
        scratch_shapes=[pltpu.VMEM((boxes, cols, width), jnp.bfloat16), pltpu.SemaphoreType.DMA((boxes // 4,))],
        compiler_params=pltpu.CompilerParams(vmem_limit_bytes=16 << 20),
        name="target_map",
    )(x, target_factor.reshape(boxes * k, width))


def per_device(bank, pick, slot_box, leaf_factor, self_factor, cross_factor, target_factor):
    x = coefs_of_device(pick, slot_box, bank, leaf_factor, self_factor, cross_factor)
    return target_map(x, target_factor)


def solution(mesh):
    in_specs = (
        P("box", "tx", None),
        P(),
        P(),
        P("box", None, None),
        P(None, "box", None, None),
        P(None, "box", None, None),
        P("box", None, None),
    )
    out_specs = P("box", "tx", None)
    return jax.shard_map(
        per_device, mesh=mesh, in_specs=in_specs, out_specs=out_specs, check_vma=False
    )
```
